32 devices in a mesh: rep: 8 (over z, x), shard: 4 (over y, core).
Axes of the slice: x: 2, y: 2, z: 4, core: 2. Of those that a mesh axis runs over, the one named last changes fastest.
Arguments:
- tokens: bfloat16 [32, 1024, 768], P(('rep', 'shard')), may hold values from -6 to 6
- lengths: int32 [32], P(('rep', 'shard')), may hold values from 512 to 1024, as said below
- cotangent: bfloat16 [32, 1024, 768], P(('rep', 'shard')), may hold values from -6 to 6
- w_query: float32 [768, 768], P('shard'), may hold values from -0.21875 to 0.21875
- b_query: float32 [768], P('shard'), may hold values from -3 to 3
- w_key: float32 [768, 768], P('shard'), may hold values from -0.21875 to 0.21875
- w_value: float32 [768, 768], P('shard'), may hold values from -0.21875 to 0.21875
- b_value: float32 [768], P('shard'), may hold values from -3 to 3
- w_output: float32 [768, 768], P('shard'), may hold values from -4 to 4
- b_output: float32 [768], P('shard'), may hold values from -3 to 3
- gain_attn: float32 [768], P('shard'), may hold values from 0.1 to 1.9
- shift_attn: float32 [768], P('shard'), may hold values from -3 to 3
- w_inner: float32 [768, 3072], P('shard'), may hold values from -0.21875 to 0.21875
- b_inner: float32 [3072], P('shard'), may hold values from -3 to 3
- w_outer: float32 [3072, 768], P('shard'), may hold values from -0.109375 to 0.109375
- b_outer: float32 [768], P('shard'), may hold values from -3 to 3
- gain_ffn: float32 [768], P('shard'), may hold values from 0.1 to 1.9
- shift_ffn: float32 [768], P('shard'), may hold values from -3 to 3
Outputs:
- layer_out: bfloat16 [32, 1024, 768], P(('rep', 'shard'))
- grad_tokens: bfloat16 [32, 1024, 768], P(('rep', 'shard'))
- grad_w_query: float32 [768, 768], P('shard')
- grad_b_query: float32 [768], P('shard')
- grad_w_key: float32 [768, 768], P('shard')
- grad_w_value: float32 [768, 768], P('shard')
- grad_b_value: float32 [768], P('shard')
- grad_w_output: float32 [768, 768], P('shard')
- grad_b_output: float32 [768], P('shard')
- grad_gain_attn: float32 [768], P('shard')
- grad_shift_attn: float32 [768], P('shard')
- grad_w_inner: float32 [768, 3072], P('shard')
- grad_b_inner: float32 [3072], P('shard')
- grad_w_outer: float32 [3072, 768], P('shard')
- grad_b_outer: float32 [768], P('shard')
- grad_gain_ffn: float32 [768], P('shard')
- grad_shift_ffn: float32 [768], P('shard')
The draws below stay inside these ranges and needn't reach their ends.
Inputs may be any that keep to these rules, and one draw needn't show every extreme that they name: `lengths`: some sequence has exactly 1024 valid tokens and some exactly half of 1024.
All inputs are finite; a program needn't handle non-finite values.
Results may differ from the reference program's by a relative error of at most 0.02.
Values may be sent and summed in bfloat16 or wider, within the bound.
A program may use at most 192 MiB of HBM per device.

```python
import math
import jax
import jax.numpy as jnp
from jax import lax

D = 768
HD = 64
FF = 3072
LEN = 1024
SEQS = 32


def draw_lengths(key, part):
    base = jax.random.randint(jax.random.fold_in(key, 11), (SEQS,), LEN // 2, LEN + 1)
    order = jax.random.permutation(jax.random.fold_in(key, 12), SEQS)
    base = base.at[order[0]].set(LEN)
    base = base.at[order[1]].set(LEN // 2)
    return base.astype(jnp.int32)


def steps_of(rng, shape, shards, low, top_value):
    loudness, own = 1.0, jax.random.fold_in(rng, 6)
    for dim, parts in shards:
        heights = jnp.exp(jax.random.uniform(jax.random.fold_in(own, dim), (parts,), jnp.float32, low / len(shards), top_value / len(shards)))
        loudness = loudness * jnp.repeat(heights, shape[dim] // parts).reshape([-1 if axis == dim else 1 for axis in range(len(shape))])
    return loudness


def bell_draw(key, shape, deviation, limit, shards=(), dtype=jnp.bfloat16):
    values = deviation * jax.random.normal(key, shape, jnp.float32)
    if shards:
        values = values * steps_of(key, shape, shards, -0.22, 0.18)
    return jnp.clip(values, -limit, limit).astype(dtype)


def setup_inputs(seed: int = 0) -> dict:
    arg_keys = jax.random.split(jax.random.key(seed), 19)
    tokens = bell_draw(arg_keys[0], (SEQS, LEN, D), 1.0, 6.0, ((0, 32),))
    lengths = draw_lengths(jax.random.fold_in(arg_keys[18], 71), 0)
    cotangent = bell_draw(arg_keys[2], (SEQS, LEN, D), 1.0, 6.0, ((0, 32),))
    w_query = bell_draw(arg_keys[3], (D, D), D ** -0.5, 0.21875, ((0, 4),), jnp.float32)
    b_query = bell_draw(arg_keys[4], (D,), 0.5, 3.0, ((0, 4),), jnp.float32)
    w_key = bell_draw(arg_keys[5], (D, D), D ** -0.5, 0.21875, ((0, 4),), jnp.float32)
    w_value = bell_draw(arg_keys[6], (D, D), D ** -0.5, 0.21875, ((0, 4),), jnp.float32)
    b_value = bell_draw(arg_keys[7], (D,), 0.5, 3.0, ((0, 4),), jnp.float32)
    w_output = bell_draw(arg_keys[8], (D, D), (max(1, D * 3 // LEN)) ** -0.5, 4.0, ((0, 4),), jnp.float32)
    b_output = bell_draw(arg_keys[9], (D,), 0.5, 3.0, ((0, 4),), jnp.float32)
    gain_attn = jnp.clip(1.0 + 0.18 * jax.random.normal(arg_keys[10], (D,), jnp.float32), 0.1, 1.9)
    shift_attn = bell_draw(arg_keys[11], (D,), 0.5, 3.0, ((0, 4),), jnp.float32)
    w_inner = bell_draw(arg_keys[12], (D, FF), D ** -0.5, 0.21875, ((0, 4),), jnp.float32)
    b_inner = bell_draw(arg_keys[13], (FF,), 0.5, 3.0, ((0, 4),), jnp.float32)
    w_outer = bell_draw(arg_keys[14], (FF, D), FF ** -0.5, 0.109375, ((0, 4),), jnp.float32)
    b_outer = bell_draw(arg_keys[15], (D,), 0.5, 3.0, ((0, 4),), jnp.float32)
    gain_ffn = jnp.clip(1.0 + 0.18 * jax.random.normal(arg_keys[16], (D,), jnp.float32), 0.1, 1.9)
    shift_ffn = bell_draw(arg_keys[17], (D,), 0.5, 3.0, ((0, 4),), jnp.float32)
    return dict(tokens=tokens, lengths=lengths, cotangent=cotangent, w_query=w_query, b_query=b_query, w_key=w_key, w_value=w_value, b_value=b_value, w_output=w_output, b_output=b_output, gain_attn=gain_attn, shift_attn=shift_attn, w_inner=w_inner, b_inner=b_inner, w_outer=w_outer, b_outer=b_outer, gain_ffn=gain_ffn, shift_ffn=shift_ffn)


EPSILON = 1e-05

@jax.custom_vjp
def low(v):
    return lax.optimization_barrier(v.astype(jnp.bfloat16)).astype(jnp.float32)

@jax.custom_vjp
def low_back(v):
    return v

def low_keep(v):
    return (low(v), None)

def low_pass(kept, grad):
    return (grad,)

def back_keep(v):
    return (v, None)

def back_low(kept, grad):
    return (low(grad),)
low.defvjp(low_keep, low_pass)
low_back.defvjp(back_keep, back_low)

def product(left, right):
    return jnp.dot(left, right, precision=lax.Precision.HIGHEST)

def normalize(row_block, gain_vec, shift_vec):
    average = lax.optimization_barrier(jnp.mean(row_block, axis=-1, keepdims=True))
    centred = row_block - average
    spread_sq = lax.optimization_barrier(jnp.mean(centred * centred, axis=-1, keepdims=True))
    return centred * lax.rsqrt(spread_sq + EPSILON) * gain_vec + shift_vec

def one_sequence(seq_rows, seq_len, rounded):
    w_query, b_query, w_key, w_value, b_value, w_output, b_output, gain_attn, shift_attn, w_inner, b_inner, w_outer, b_outer, gain_ffn, shift_ffn = rounded
    positions = jnp.arange(seq_rows.shape[0])
    live_rows = (positions < seq_len).astype(jnp.float32)
    queries = low(low_back(product(seq_rows, w_query) + b_query))
    keys_in = low(low_back(product(seq_rows, w_key)))
    values_in = low(low_back(product(seq_rows, w_value) + b_value))
    head_shape = (seq_rows.shape[0], seq_rows.shape[1] // HD, HD)
    scores = jnp.einsum('qhd,khd->hqk', queries.reshape(head_shape), keys_in.reshape(head_shape), precision=lax.Precision.HIGHEST) * (1.0 / math.sqrt(HD))
    scores = low_back(scores)
    scores = jnp.where(live_rows[None, None, :] > 0, scores, -1000000000.0)
    top_score = lax.optimization_barrier(jnp.max(scores, axis=-1, keepdims=True))
    exponent = jnp.exp(scores - top_score)
    row_sum = lax.optimization_barrier(jnp.sum(exponent, axis=-1, keepdims=True))
    attn_prob = exponent / row_sum
    attended = jnp.einsum('hqk,khd->qhd', low(attn_prob), values_in.reshape(head_shape), precision=lax.Precision.HIGHEST).reshape(seq_rows.shape)
    attended = low(low_back(attended))
    branch = low_back(product(attended, w_output) + b_output)
    first_out = normalize(seq_rows + branch, gain_attn, shift_attn)
    hidden = low_back(product(low(first_out), w_inner) + b_inner)
    activated = low(jax.nn.gelu(hidden, approximate=False))
    second = low_back(product(activated, w_outer) + b_outer)
    return normalize(first_out + second, gain_ffn, shift_ffn) * live_rows[:, None]

def reference(tokens, lengths, cotangent, w_query, b_query, w_key, w_value, b_value, w_output, b_output, gain_attn, shift_attn, w_inner, b_inner, w_outer, b_outer, gain_ffn, shift_ffn):
    params = (w_query, b_query, w_key, w_value, b_value, w_output, b_output, gain_attn, shift_attn, w_inner, b_inner, w_outer, b_outer, gain_ffn, shift_ffn)
    seq_inputs = tokens.astype(jnp.float32)
    cot_rows = cotangent.astype(jnp.float32)

    def forward(seq_inputs, params):
        rounded = tuple((low(master) for master in params))

        def per_seq(carry_in, pieces):
            seq_rows, seq_len = pieces
            return (carry_in, jax.checkpoint(one_sequence)(seq_rows, seq_len, rounded))
        carry_out, outputs = lax.scan(per_seq, jnp.zeros((), jnp.float32), (seq_inputs, lengths))
        return outputs
    outputs, pullback = jax.vjp(forward, seq_inputs, params)
    grad_inputs, grad_params = pullback(cot_rows)
    factor = 1.0 / math.sqrt(SEQS * LEN)
    return (outputs.astype(jnp.bfloat16), grad_inputs.astype(jnp.bfloat16), grad_params[0] * factor, grad_params[1] * factor, grad_params[2] * factor, grad_params[3] * factor, grad_params[4] * factor, grad_params[5] * factor, grad_params[6] * factor, grad_params[7] * factor, grad_params[8] * factor, grad_params[9] * factor, grad_params[10] * factor, grad_params[11] * factor, grad_params[12] * factor, grad_params[13] * factor, grad_params[14] * factor)
```

```python
import functools
import math

import jax
import jax.numpy as jnp
from jax import lax
from jax.experimental import pallas as pl
from jax.experimental.pallas import tpu as pltpu
from jax.sharding import PartitionSpec as P

HD = 64
EPS = 1e-5
NEG = -1e9
BF = jnp.bfloat16
F32 = jnp.float32
RB = 256
KB = 256
PADW = 256
MESH = pl.DeviceIdType.MESH
VMEM_LIMIT = 64000 * 1024
INV_SQRT2 = 1.0 / math.sqrt(2.0)
INV_SQRT2PI = 1.0 / math.sqrt(2.0 * math.pi)


def sds(*shape, dtype=BF):
    return jax.ShapeDtypeStruct(shape, dtype)


def dot(a, b, ca=1, cb=0, precision=None):
    return lax.dot_general(a, b, (((ca,), (cb,)), ((), ())), preferred_element_type=F32, precision=precision)


def colsum(a):
    return jnp.sum(a.astype(F32), axis=0, keepdims=True)


def vm():
    return pl.BlockSpec(memory_space=pltpu.VMEM)


def hbm():
    return pl.BlockSpec(memory_space=pl.ANY)


def smem():
    return pl.BlockSpec(memory_space=pltpu.SMEM)


def place(shards, width, dim):
    row = lax.broadcasted_iota(jnp.int32, (shards * PADW, dim), 0)
    col = lax.broadcasted_iota(jnp.int32, (shards * PADW, dim), 1)
    return jnp.where((row % PADW < width) & (row // PADW * width + row % PADW == col), 1.0, 0.0)


def whole_vectors(vbuf, flat, vec, shards, dim, chunks):
    flat[...] = jnp.zeros_like(flat)
    for b in range(shards):
        flat[0:8, b * PADW : (b + 1) * PADW] = vbuf[b, 0:8, :]
        for j in range(chunks):
            q, blk = divmod(b * chunks + j, shards)
            flat[8 + q : 9 + q, blk * PADW : (blk + 1) * PADW] = vbuf[b, 8 + j : 9 + j, :]
    sel = place(shards, dim // shards, dim).astype(BF)
    vec[...] = dot(flat[...].astype(BF), sel)


def split_vectors(sums, flat, sbuf, shards, dim, chunks):
    sel = place(shards, dim // shards, dim)
    flat[...] = dot(sums[...], sel, 1, 1, precision=lax.Precision.HIGHEST)
    for b in range(shards):
        sbuf[b, 0:8, :] = flat[0:8, b * PADW : (b + 1) * PADW]
        sbuf[b, 8:16, :] = jnp.zeros((8, PADW), F32)
        for j in range(chunks):
            q, blk = divmod(b * chunks + j, shards)
            sbuf[b, 8 + j : 9 + j, :] = flat[8 + q : 9 + q, blk * PADW : (blk + 1) * PADW]


def other_core(s):
    return s + 1 - 2 * lax.rem(s, 2)


def gather_kernel(S, R, dims, mq, mk, mv, mo, m1, m2, vp, oq, ok, ov, oo, o1, o2, vec,
                  stage, gq, gk, gv, go, g1, g2, vbuf, flat,
                  lsem, osem, cs, cr, ys, yr, xs, xr, fs, fr, gs, gr, vs, vr):
    D, FFW = dims
    w, nc = D // S, FFW // D
    r, s = lax.axis_index("rep"), lax.axis_index("shard")
    core = other_core(s)
    twin = other_core(r)
    half = lax.rem(r, 2)

    def masters(u):
        if u < 4:
            return (mq, mk, mv, mo)[u]
        if u < 4 + nc:
            return m1.at[:, (u - 4) * D : (u - 3) * D]
        return m2.at[(u - 4 - nc) * w : (u - 3 - nc) * w, :]

    def view(u, owner, part=None):
        cols = pl.ds(0, D) if part is None else pl.ds(pl.multiple_of(part * (D // 2), 128), D // 2)
        if u < 4:
            return (gq, gk, gv, go)[u].at[pl.ds(pl.multiple_of(owner * w, 8), w), cols]
        if u < 4 + nc:
            base = (u - 4) * D
            cols = pl.ds(base, D) if part is None else pl.ds(pl.multiple_of(base + part * (D // 2), 128), D // 2)
            return g1.at[pl.ds(pl.multiple_of(owner * w, 8), w), cols]
        return g2.at[pl.ds(pl.multiple_of(owner * (nc * w) + (u - 4 - nc) * w, 8), w), cols]

    n = 4 + 2 * nc
    loads = [pltpu.make_async_copy(masters(u), stage.at[u], lsem.at[u]) for u in range(n)]
    for c in loads:
        c.start()

    barrier = pltpu.get_barrier_semaphore()
    peers = [(r, lax.rem(s + j, S)) for j in range(1, S)] + [(twin, s)]
    for p in peers:
        pl.semaphore_signal(barrier, inc=1, device_id=p, device_id_type=MESH)
    pl.semaphore_wait(barrier, len(peers))

    def remote(src, dst, ssem, rsem, dev):
        return pltpu.make_async_remote_copy(src_ref=src, dst_ref=dst, send_sem=ssem, recv_sem=rsem, device_id=dev, device_id_type=MESH)

    vbuf[s] = vp[...].astype(BF).astype(F32)
    vcopies = [remote(vbuf.at[s], vbuf.at[s], vs.at[j - 1], vr.at[j - 1], (r, lax.rem(s + j, S))) for j in range(1, S)]

    across = range(1, S // 2)
    core_copy, y_copy, x_copy, f_copy, g_copy = {}, {}, {}, {}, {}

    def begin(u):
        loads[u].wait()
        view(u, s)[...] = stage[u].astype(BF)
        for j in across:
            mine = view(u, s, half)
            y_copy[u, j] = remote(mine, mine, ys.at[u, j - 1], yr.at[u, j - 1], (r, lax.rem(s + 2 * j, S)))
            y_copy[u, j].start()
        mine = view(u, s)
        core_copy[u] = remote(mine, mine, cs.at[u], cr.at[u], (r, core))
        core_copy[u].start()

    def relay_y(u):
        for j in across:
            owner = lax.rem(s + S - 2 * j, S)
            y_copy[u, j].wait_recv()
            got = view(u, owner, half)
            x_copy[u, j] = remote(got, got, xs.at[u, j - 1], xr.at[u, j - 1], (twin, s))
            x_copy[u, j].start()
            f_copy[u, j] = remote(got, got, fs.at[u, j - 1], fr.at[u, j - 1], (r, core))
            f_copy[u, j].start()

    def relay_x(u):
        for j in across:
            owner = lax.rem(s + S - 2 * j, S)
            x_copy[u, j].wait_recv()
            got = view(u, owner, 1 - half)
            g_copy[u, j] = remote(got, got, gs.at[u, j - 1], gr.at[u, j - 1], (r, core))
            g_copy[u, j].start()

    def finish(u):
        core_copy[u].wait_recv()
        for j in across:
            f_copy[u, j].wait_recv()
            g_copy[u, j].wait_recv()

    def drain(u):
        core_copy[u].wait_send()
        for j in across:
            y_copy[u, j].wait_send()
            x_copy[u, j].wait_send()
            f_copy[u, j].wait_send()
            g_copy[u, j].wait_send()

    begin(0)
    for c in vcopies:
        c.start()
    begin(1)
    for u in range(n):
        if u + 2 < n:
            begin(u + 2)
        relay_y(u)
        if u >= 1:
            relay_x(u - 1)
    relay_x(n - 1)
    for c in vcopies:
        c.wait()
    whole_vectors(vbuf, flat, vec, S, D, nc)
    for u in range(n):
        finish(u)
    outs = [pltpu.make_async_copy(a, b, osem.at[i]) for i, (a, b) in enumerate(((gq, oq), (gk, ok), (gv, ov), (go, oo), (g1, o1), (g2, o2)))]
    for c in outs:
        c.start()
    for u in range(n):
        drain(u)
    for c in outs:
        c.wait()


def gather_weights(S, R, wq, wk, wv, wo, w1, w2, vp):
    w, FFW = w1.shape
    D = w * S
    nc = FFW // D
    n = 4 + 2 * nc
    a = max(1, S // 2 - 1)
    dma = pltpu.SemaphoreType.DMA
    return pl.pallas_call(
        functools.partial(gather_kernel, S, R, (D, FFW)),
        out_shape=[sds(D, D)] * 4 + [sds(D, FFW), sds(FFW, D), sds(16, D, dtype=F32)],
        in_specs=[hbm()] * 6 + [vm()],
        out_specs=[hbm()] * 6 + [vm()],
        scratch_shapes=[pltpu.VMEM((n, w, D), F32)] + [pltpu.VMEM((D, D), BF)] * 4
        + [pltpu.VMEM((D, FFW), BF), pltpu.VMEM((FFW, D), BF), pltpu.VMEM((S, 16, PADW), F32), pltpu.VMEM((16, S * PADW), F32)]
        + [dma((n,)), dma((6,)), dma((n,)), dma((n,))] + [dma((n, a))] * 8 + [dma((S - 1,))] * 2,
        compiler_params=pltpu.CompilerParams(collective_id=0, has_side_effects=True, vmem_limit_bytes=VMEM_LIMIT),
    )(wq, wk, wv, wo, w1, w2, vp)


def attn_fwd_kernel(x, wq, wk, wv, vec, ln, q, k, v, ot, lse, st, mx, ka, qa, vt):
    rows, D = x.shape
    pairs = D // (2 * HD)

    def project(g, _):
        cols = pl.ds(pl.multiple_of(g * 256, 256), 256)
        xx = x[...]
        q[:, cols] = ((dot(xx, wq[:, cols]) + vec[0:1, cols]).astype(BF) * 0.125).astype(BF)
        k[:, cols] = dot(xx, wk[:, cols]).astype(BF)
        v[:, cols] = (dot(xx, wv[:, cols]) + vec[1:2, cols]).astype(BF)
        return 0

    lax.fori_loop(0, D // 256, project, 0)
    bias = jnp.where(lax.broadcasted_iota(jnp.int32, (rows, 128), 0) < ln[0], 0.0, NEG)
    lane = lax.broadcasted_iota(jnp.int32, (rows, 128), 1)
    QT = 256

    def prep(p, h):
        cols = pl.ds(pl.multiple_of(p * 128, 128), 128)
        mine = (lane < HD) if h == 0 else (lane >= HD)
        ka[h] = jnp.where(mine, k[:, cols].astype(F32), jnp.where(lane == (HD if h == 0 else 0), bias, 0.0)).astype(BF)
        qa[h] = jnp.where(mine, q[:, cols].astype(F32), 1.0).astype(BF)

    def scores(h, t):
        ts = slice(t * QT, (t + 1) * QT)
        sc = dot(ka[h], qa[h, ts, :], 1, 1)
        st[h, :, ts] = sc
        mx[h, 0:1, ts] = jnp.max(sc, axis=0, keepdims=True)

    def weigh(p, h, t):
        ts = slice(t * QT, (t + 1) * QT)
        m = mx[h, 0:1, ts]
        e = jnp.exp(st[h, :, ts] - m).astype(BF)
        o = dot(vt[h], e)
        total = o[HD : HD + 1, :]
        ot[pl.ds(pl.multiple_of(p * 128 + h * HD, HD), HD), ts] = (o[:HD, :] / total).astype(BF)
        lse[p * 2 + h, :, ts] = m + jnp.log(total)

    def prep_values(p, h):
        cols = pl.ds(pl.multiple_of(p * 128, 128), 128)
        vt[h, 0:HD, :] = v[:, cols].T[h * HD : (h + 1) * HD, :]
        vt[h, HD : HD + 16, :] = jnp.ones((16, rows), BF)

    prep(0, 0)
    for t in range(rows // QT):
        scores(0, t)

    def body(p, _):
        nxt = lax.rem(p + 1, pairs)
        for h in range(2):
            prep(p if h == 0 else nxt, 1 - h)
            prep_values(p, h)
            for t in range(rows // QT):
                scores(1 - h, t)
                weigh(p, h, t)
        return 0

    lax.fori_loop(0, pairs, body, 0)


def attn_fwd(x, wq, wk, wv, vec, ln):
    rows, D = x.shape
    return pl.pallas_call(
        attn_fwd_kernel,
        out_shape=[sds(rows, D)] * 3 + [sds(D, rows), sds(D // HD, 1, rows, dtype=F32)],
        in_specs=[vm()] * 5 + [smem()],
        out_specs=[vm()] * 5,
        scratch_shapes=[pltpu.VMEM((2, rows, rows), F32), pltpu.VMEM((2, 8, rows), F32)] + [pltpu.VMEM((2, rows, 128), BF)] * 2
        + [pltpu.VMEM((2, HD + 16, rows), BF)],
        compiler_params=pltpu.CompilerParams(vmem_limit_bytes=VMEM_LIMIT),
    )(x, wq, wk, wv, vec, ln)


def gelu_parts(h):
    cdf = 0.5 + 0.5 * lax.erf(h * INV_SQRT2)
    pdf = jnp.exp(h * h * (-0.5)) * INV_SQRT2PI
    return h * cdf, cdf + h * pdf


def ln_stats(r):
    c = r - jnp.mean(r, axis=-1, keepdims=True)
    rs = lax.rsqrt(jnp.mean(c * c, axis=-1, keepdims=True) + EPS)
    return c * rs, rs


def ln_back(dy, xh, rs, gain):
    dx = dy * gain
    a = jnp.mean(dx, axis=-1, keepdims=True)
    b = jnp.mean(dx * xh, axis=-1, keepdims=True)
    return rs * (dx - a - xh * b)


def ffn_kernel(x, cot, ot, wo, w1, w2, vec, ln, y, do, dr1, dd, sums, dw2, dw1, dwo, g, dh, x1b, df, da, gp):
    rows, D = x.shape
    nc = w1.shape[1] // D
    heads = D // HD
    sums[...] = jnp.zeros_like(sums)

    def block(i, _):
        r0 = pl.multiple_of(i * RB, RB)
        rr = pl.ds(r0, RB)
        live = (lax.broadcasted_iota(jnp.int32, (RB, 1), 0) + r0 < ln[0]).astype(F32)
        r1 = x[rr, :].astype(F32) + dot(ot[:, rr], wo[...], 0, 0) + vec[2:3, :]
        xh1, rs1 = ln_stats(r1)
        x1 = xh1 * vec[3:4, :] + vec[4:5, :]
        xb = x1.astype(BF)
        x1b[rr, :] = xb
        r2 = x1 + vec[5:6, :]
        for c in range(nc):
            cs = slice(c * D, (c + 1) * D)
            act, der = gelu_parts(dot(xb, w1[:, cs]) + vec[8 + c : 9 + c, :])
            act = act.astype(BF)
            g[rr, cs] = act
            gp[:, cs] = der
            r2 = r2 + dot(act, w2[cs, :])
        xh2, rs2 = ln_stats(r2)
        y[rr, :] = ((xh2 * vec[6:7, :] + vec[7:8, :]) * live).astype(BF)
        dy = cot[rr, :].astype(F32) * live
        sums[6:7, :] += colsum(dy * xh2)
        sums[7:8, :] += colsum(dy)
        dr2 = ln_back(dy, xh2, rs2, vec[6:7, :])
        dfb = dr2.astype(BF)
        df[rr, :] = dfb
        sums[5:6, :] += colsum(dfb)
        dx1 = dr2
        for c in range(nc):
            cs = slice(c * D, (c + 1) * D)
            dhb = (dot(dfb, w2[cs, :], 1, 1) * gp[:, cs]).astype(BF)
            dh[rr, cs] = dhb
            sums[8 + c : 9 + c, :] += colsum(dhb)
            dx1 = dx1 + dot(dhb, w1[:, cs], 1, 1)
        sums[3:4, :] += colsum(dx1 * xh1)
        sums[4:5, :] += colsum(dx1)
        d1 = ln_back(dx1, xh1, rs1, vec[3:4, :])
        dr1[rr, :] = d1
        dab = d1.astype(BF)
        da[rr, :] = dab
        sums[2:3, :] += colsum(dab)
        do[rr, :] = dot(dab, wo[...], 1, 1).astype(BF)
        dot_t = dot(wo[...], dab, 1, 1).astype(BF).astype(F32) * ot[:, rr].astype(F32)
        for h in range(heads):
            dd[h, :, rr] = jnp.sum(dot_t[h * HD : (h + 1) * HD, :], axis=0, keepdims=True)
        return 0

    lax.fori_loop(0, rows // RB, block, 0)
    for c in range(nc):
        cs = slice(c * D, (c + 1) * D)
        dw2[cs, :] = dot(g[:, cs], df[...], 0, 0).astype(BF)
        dw1[:, cs] = dot(x1b[...], dh[:, cs], 0, 0).astype(BF)
    dwo[...] = dot(ot[...], da[...]).astype(BF)


def ffn(x, cot, ot, wo, w1, w2, vec, ln):
    rows, D = x.shape
    FFW = w1.shape[1]
    return pl.pallas_call(
        ffn_kernel,
        out_shape=[sds(rows, D), sds(rows, D), sds(rows, D, dtype=F32), sds(D // HD, 1, rows, dtype=F32), sds(16, D, dtype=F32),
                   sds(FFW, D), sds(D, FFW), sds(D, D)],
        in_specs=[vm()] * 7 + [smem()],
        out_specs=[vm()] * 8,
        scratch_shapes=[pltpu.VMEM((rows, FFW), BF)] * 2 + [pltpu.VMEM((rows, D), BF)] * 3 + [pltpu.VMEM((RB, FFW), F32)],
        compiler_params=pltpu.CompilerParams(vmem_limit_bytes=VMEM_LIMIT),
    )(x, cot, ot, wo, w1, w2, vec, ln)


def attn_bwd_kernel(q, k, v, do, lse, dd, x, dr1, wq, wk, wv, sums_in, ln, dx, dwq, dwk, dwv, sums,
                    dqt, dk, dv, st, dp, ka, qa, va, kt, hk, hv):
    rows, D = x.shape
    pairs = D // (2 * HD)
    nk = rows // KB
    bias = jnp.where(lax.broadcasted_iota(jnp.int32, (rows, 128), 0) < ln[0], 0.0, NEG)
    lane = lax.broadcasted_iota(jnp.int32, (rows, 128), 1)
    laneb = lax.broadcasted_iota(jnp.int32, (KB, 128), 1)

    def at(p):
        return pl.ds(pl.multiple_of(p * 128, 128), 128)

    def prep(p, h):
        mine = (lane < HD) if h == 0 else (lane >= HD)
        kp = k[:, at(p)]
        ka[h] = jnp.where(mine, kp.astype(F32), jnp.where(lane == (HD if h == 0 else 0), bias, 0.0)).astype(BF)
        qa[h] = jnp.where(mine, q[:, at(p)].astype(F32), 1.0).astype(BF)
        va[h] = jnp.where(mine, v[:, at(p)].astype(F32), 0.0).astype(BF)
        kt[h] = kp.T[h * HD : (h + 1) * HD, :]

    def first(p, h, i, b):
        ks = slice(i * KB, (i + 1) * KB)
        st[b] = dot(ka[h, ks, :], qa[h], 1, 1)
        dp[b] = dot(va[h, ks, :], do[:, at(p)], 1, 1)

    def second(p, h, i, b):
        ks = slice(i * KB, (i + 1) * KB)
        e = jnp.exp(st[b] - lse[p * 2 + h])
        ds = (e * (dp[b] - dd[p * 2 + h])).astype(BF)
        dvb = dot(e.astype(BF), do[:, at(p)])
        dkb = dot(ds, q[:, at(p)])
        if h == 0:
            hv[ks, :] = dvb
            hk[ks, :] = dkb
        else:
            dv[ks, at(p)] = jnp.where(laneb < HD, hv[ks, :], dvb).astype(BF)
            dk[ks, at(p)] = jnp.where(laneb < HD, hk[ks, :], dkb).astype(BF)
        return dot(kt[h, :, ks], ds)

    prep(0, 0)
    first(0, 0, 0, 0)

    def body(p, _):
        nxt = lax.rem(p + 1, pairs)
        blk = 0
        for h in range(2):
            prep(p if h == 0 else nxt, 1 - h)
            acc = None
            for i in range(nk):
                b = blk % 2
                if i < nk - 1:
                    first(p, h, i + 1, 1 - b)
                else:
                    first(p if h == 0 else nxt, 1 - h, 0, 1 - b)
                part = second(p, h, i, b)
                acc = part if acc is None else acc + part
                blk += 1
            dqt[pl.ds(pl.multiple_of(p * 128 + h * HD, HD), HD), :] = (acc * 0.125).astype(BF)
        return 0

    lax.fori_loop(0, pairs, body, 0)
    sums[...] = sums_in[...]
    ones = jnp.ones((8, rows), BF)
    sums[0:1, :] = dot(ones, dqt[...], 1, 1)[0:1, :]
    sums[1:2, :] = dot(ones, dv[...])[0:1, :]
    dwq[...] = dot(x[...], dqt[...], 0, 1).astype(BF)
    dwk[...] = dot(x[...], dk[...], 0, 0).astype(BF)
    dwv[...] = dot(x[...], dv[...], 0, 0).astype(BF)
    for i in range(rows // RB):
        rr = slice(i * RB, (i + 1) * RB)
        dx[rr, :] = (dr1[rr, :] + dot(dqt[:, rr], wq[...], 0, 1) + dot(dk[rr, :], wk[...], 1, 1) + dot(dv[rr, :], wv[...], 1, 1)).astype(BF)


def attn_bwd(q, k, v, do, lse, dd, x, dr1, wq, wk, wv, sums, ln):
    rows, D = x.shape
    return pl.pallas_call(
        attn_bwd_kernel,
        out_shape=[sds(rows, D)] + [sds(D, D)] * 3 + [sds(16, D, dtype=F32)],
        in_specs=[vm()] * 12 + [smem()],
        out_specs=[vm()] * 5,
        scratch_shapes=[pltpu.VMEM((D, rows), BF), pltpu.VMEM((rows, D), BF), pltpu.VMEM((rows, D), BF)]
        + [pltpu.VMEM((2, KB, rows), F32)] * 2 + [pltpu.VMEM((2, rows, 128), BF)] * 3 + [pltpu.VMEM((2, HD, rows), BF)]
        + [pltpu.VMEM((rows, 128), F32)] * 2,
        compiler_params=pltpu.CompilerParams(vmem_limit_bytes=VMEM_LIMIT),
    )(q, k, v, do, lse, dd, x, dr1, wq, wk, wv, sums, ln)


def reduce_kernel(S, R, dims, dq, dk, dv, do, d1, d2, sums, fin_out, small,
                  own, far, mid, got, fin, tosend, sbuf, flat, srecv, sacc, trecv,
                  lsem, fsem, osem, s1, r1, s2, r2, s3, r3, s4, r4, vs1, vr1, vs2, vr2):
    D, FFW = dims
    w, nc = D // S, FFW // D
    n = 4 + 2 * nc
    piece = w // R
    r, s = lax.axis_index("rep"), lax.axis_index("shard")
    c, y = lax.rem(s, 2), s // 2
    core = other_core(s)

    def block(u, b):
        if u < nc:
            return d2.at[pl.ds(pl.multiple_of(b * (nc * w) + u * w, 8), w), :]
        if u < 2 * nc:
            return d1.at[pl.ds(pl.multiple_of(b * w, 8), w), (u - nc) * D : (u - nc + 1) * D]
        return (do, dq, dk, dv)[u - 2 * nc].at[pl.ds(pl.multiple_of(b * w, 8), w), :]

    def remote(src, dst, ssem, rsem, dev):
        return pltpu.make_async_remote_copy(src_ref=src, dst_ref=dst, send_sem=ssem, recv_sem=rsem, device_id=dev, device_id_type=MESH)

    barrier = pltpu.get_barrier_semaphore()
    peers = [(r, lax.rem(s + j, S)) for j in range(1, S)] + [(lax.rem(r + j, R), s) for j in range(1, R)]
    for p in peers:
        pl.semaphore_signal(barrier, inc=1, device_id=p, device_id_type=MESH)
    pl.semaphore_wait(barrier, len(peers))

    held = {}

    def keep(*copies):
        for cp in copies:
            cp.start()
        return copies

    def stage1(u):
        held["own", u] = keep(*[pltpu.make_async_copy(block(u, 2 * kk + c), own.at[u, kk], lsem.at[u, kk]) for kk in range(S // 2)])
        held["s1", u] = keep(*[remote(block(u, 2 * kk + 1 - c), far.at[u, kk], s1.at[u, kk], r1.at[u, kk], (r, core)) for kk in range(S // 2)])

    def stage2(u):
        for cp in held["own", u]:
            cp.wait()
        for cp in held["s1", u]:
            cp.wait_recv()
        for kk in range(S // 2):
            own[u, kk] = (own[u, kk].astype(F32) + far[u, kk].astype(F32)).astype(BF)
        held["s2", u] = keep(*[
            remote(own.at[u, lax.rem(y + j, S // 2)], mid.at[u, j - 1], s2.at[u, j - 1], r2.at[u, j - 1], (r, lax.rem(s + 2 * j, S)))
            for j in range(1, S // 2)])

    def stage3(u):
        for cp in held["s2", u]:
            cp.wait_recv()
        for i in range(R):
            rows = slice(i * piece, (i + 1) * piece)
            acc = own[u, y, rows, :].astype(F32)
            for j in range(1, S // 2):
                acc = acc + mid[u, j - 1, rows, :].astype(F32)
            tosend[u, i] = acc.astype(BF)
        held["s3", u] = keep(*[
            remote(tosend.at[u, lax.rem(r + j, R)], got.at[u, j - 1], s3.at[u, j - 1], r3.at[u, j - 1], (lax.rem(r + j, R), s))
            for j in range(1, R)])

    def stage4(u):
        acc = tosend[u, r].astype(F32)
        for j in range(1, R):
            held["s3", u][j - 1].wait_recv()
            acc = acc + got[u, j - 1].astype(F32)
        fin[u, r] = acc.astype(BF)
        held["s4", u] = keep(*[
            remote(fin.at[u, r], fin.at[u, r], s4.at[u, j - 1], r4.at[u, j - 1], (lax.rem(r + j, R), s)) for j in range(1, R)])

    def stage5(u):
        for cp in held["s4", u]:
            cp.wait_recv()
        held["out", u] = keep(pltpu.make_async_copy(fin.at[u], fin_out.at[u], osem.at[u]))

    split_vectors(sums, flat, sbuf, S, D, nc)
    v1 = keep(*[remote(sbuf.at[lax.rem(s + j, S)], srecv.at[j - 1], vs1.at[j - 1], vr1.at[j - 1], (r, lax.rem(s + j, S))) for j in range(1, S)])
    stages = (stage1, stage2, stage3, stage4, stage5)
    v2 = ()
    for t in range(n + 4):
        for i, f in enumerate(stages):
            if 0 <= t - i < n:
                f(t - i)
        if t == 1:
            acc = sbuf[s]
            for j in range(1, S):
                v1[j - 1].wait_recv()
                acc = acc + srecv[j - 1]
            sacc[...] = acc
            v2 = keep(*[remote(sacc, trecv.at[j - 1], vs2.at[j - 1], vr2.at[j - 1], (lax.rem(r + j, R), s)) for j in range(1, R)])
    acc = sacc[...]
    for j in range(1, R):
        v2[j - 1].wait_recv()
        acc = acc + trecv[j - 1]
    small[...] = acc
    for cp in v1 + v2:
        cp.wait_send()
    for u in range(n):
        for key in ("s1", "s2", "s3", "s4"):
            for cp in held[key, u]:
                cp.wait_send()
        for cp in held["out", u]:
            cp.wait()


def reduce_grads(S, R, dq, dk, dv, do, d1, d2, sums):
    D, FFW = d1.shape
    w, nc = D // S, FFW // D
    n = 4 + 2 * nc
    piece = w // R
    h = S // 2
    a = max(1, h - 1)
    dma = pltpu.SemaphoreType.DMA
    return pl.pallas_call(
        functools.partial(reduce_kernel, S, R, (D, FFW)),
        out_shape=[sds(n, R, piece, D), sds(16, PADW, dtype=F32)],
        in_specs=[hbm()] * 6 + [vm()],
        out_specs=[hbm(), vm()],
        scratch_shapes=[pltpu.VMEM((n, h, w, D), BF), pltpu.VMEM((n, h, w, D), BF), pltpu.VMEM((n, a, w, D), BF),
                        pltpu.VMEM((n, R - 1, piece, D), BF), pltpu.VMEM((n, R, piece, D), BF), pltpu.VMEM((n, R, piece, D), BF),
                        pltpu.VMEM((S, 16, PADW), F32), pltpu.VMEM((16, S * PADW), F32), pltpu.VMEM((S - 1, 16, PADW), F32),
                        pltpu.VMEM((16, PADW), F32), pltpu.VMEM((R - 1, 16, PADW), F32)]
        + [dma((n, h)), dma((1,)), dma((n,)), dma((n, h)), dma((n, h)), dma((n, a)), dma((n, a))]
        + [dma((n, R - 1))] * 4 + [dma((S - 1,))] * 2 + [dma((R - 1,))] * 2,
        compiler_params=pltpu.CompilerParams(collective_id=1, has_side_effects=True, vmem_limit_bytes=VMEM_LIMIT),
    )(dq, dk, dv, do, d1, d2, sums)


def local(S, R, tokens, lengths, cotangent, w_query, b_query, w_key, w_value, b_value, w_output, b_output, gain_attn,
          shift_attn, w_inner, b_inner, w_outer, b_outer, gain_ffn, shift_ffn):
    rows, D = tokens.shape[1:]
    FFW = w_inner.shape[1]
    w, nc = D // S, FFW // D
    x, cot = tokens.reshape(rows, D), cotangent.reshape(rows, D)
    small = jnp.concatenate([b_query, b_value, b_output, gain_attn, shift_attn, b_outer, gain_ffn, shift_ffn, b_inner])
    vp = jnp.pad(small.reshape(8 + nc, w), ((0, 8 - nc), (0, PADW - w)))
    fused = (w % R == 0) and (w // R) % 8 == 0
    if fused:
        wq, wk, wv, wo, w1, w2, vec = gather_weights(S, R, w_query, w_key, w_value, w_output, w_inner, w_outer, vp)
    else:
        wq, wk, wv, wo, w1, w2 = (
            lax.all_gather(m.astype(BF), "shard", axis=0, tiled=True) for m in (w_query, w_key, w_value, w_output, w_inner, w_outer))
        parts = lax.all_gather(small.astype(BF).reshape(8 + nc, w), "shard", axis=0)
        head = jnp.transpose(parts[:, :8], (1, 0, 2)).reshape(8, D)
        vec = jnp.pad(jnp.concatenate([head, parts[:, 8:].reshape(nc, D)]).astype(F32), ((0, 8 - nc), (0, 0)))
    q, k, v, ot, lse = attn_fwd(x, wq, wk, wv, vec, lengths)
    y, do, dr1, dd, sums, dw2, dw1, dwo = ffn(x, cot, ot, wo, w1, w2, vec, lengths)
    dx, dwq, dwk, dwv, sums = attn_bwd(q, k, v, do, lse, dd, x, dr1, wq, wk, wv, sums, lengths)
    factor = 1.0 / math.sqrt(rows * R * S)
    if fused:
        fin, sm = reduce_grads(S, R, dwq, dwk, dwv, dwo, dw1, dw2, sums)
        fin = fin.reshape(4 + 2 * nc, w, D).astype(F32) * factor
        sm = sm * factor
        g2 = fin[:nc].reshape(nc * w, D)
        g1 = jnp.transpose(fin[nc : 2 * nc], (1, 0, 2)).reshape(w, FFW)
        go, gq, gk, gv = (fin[2 * nc + i] for i in range(4))
        vecs = [sm[i, :w] for i in range(8)]
        gb1 = sm[8 : 8 + nc, :w].reshape(nc * w)
    else:
        def share(t):
            t = lax.psum_scatter(t.astype(BF), "shard", scatter_dimension=0, tiled=True)
            return lax.psum(t, "rep").astype(F32) * factor

        gq, gk, gv, go, g1, g2 = (share(t) for t in (dwq, dwk, dwv, dwo, dw1, dw2))
        vecs = [share(sums[i]) for i in range(8)]
        gb1 = share(sums[8 : 8 + nc].reshape(FFW))
    gbq, gbv, gbo, gg1, gc1, gb2, gg2, gc2 = vecs
    return (y.reshape(tokens.shape), dx.reshape(tokens.shape), gq, gbq, gk, gv, gbv, go, gbo, gg1, gc1, g1, gb1, g2, gb2, gg2, gc2)


def solution(mesh):
    R, S = mesh.shape["rep"], mesh.shape["shard"]
    seq, mat, row = P(("rep", "shard"), None, None), P("shard", None), P("shard")
    params = (mat, row, mat, mat, row, mat, row, row, row, mat, row, mat, row, row, row)
    return jax.shard_map(functools.partial(local, S, R), mesh=mesh, in_specs=(seq, P(("rep", "shard")), seq) + params,
                         out_specs=(seq, seq) + params, check_vma=False)
```
